512 devices in a mesh: dp: 8 (over z_lo, core), expert: 64 (over x, y, z_hi).
Axes of the slice: x: 4, y: 8, z: 8 (z_hi: 2, z_lo: 4; z = z_hi * 4 + z_lo), core: 2. Of those that a mesh axis runs over, the one named last changes fastest.
Arguments:
- tokens: bfloat16 [10240, 2048], P('expert', 'dp'), may hold values from -6 to 6
- grad_out: bfloat16 [10240, 2048], P('expert', 'dp'), may hold values from -6 to 6
- expert_ids: int32 [10240, 2], P('expert'), may hold values from 0 to 63, all different within a row; in each aligned block of 160 rows (0 to 159, 160 to 319, ...) at most 7 rows name the same one
- gate_probs: float32 [10240, 2], P('expert'), may hold values from 0.1 to 1
- gate_weight: bfloat16 [64, 2048, 1024], P('expert', None, 'dp'), may hold values from -0.125 to 0.125
- up_weight: bfloat16 [64, 2048, 1024], P('expert', None, 'dp'), may hold values from -0.125 to 0.125
- down_weight: bfloat16 [64, 1024, 2048], P('expert', 'dp'), may hold values from -0.1875 to 0.1875
Outputs:
- layer_out: bfloat16 [10240, 2048], P('expert', 'dp')
- grad_tokens: bfloat16 [10240, 2048], P('expert', 'dp')
- grad_gate_weight: bfloat16 [64, 2048, 1024], P('expert', None, 'dp')
- grad_up_weight: bfloat16 [64, 2048, 1024], P('expert', None, 'dp')
- grad_down_weight: bfloat16 [64, 1024, 2048], P('expert', 'dp')
The draws below stay inside these ranges and needn't reach their ends.
Inputs may be any that keep to these rules, and one draw needn't show every extreme that they name: `expert_ids`: the two ids of a row differ. In every aligned block of 160 rows no expert is named by more than 7 rows, a bound that some block reaches.
All inputs are finite; a program needn't handle non-finite values.
Results may differ from the reference program's by a relative error of at most 0.015.
Values may be sent and summed in bfloat16 or wider, within the bound.
No kernel may reach another device: no remote copies, remote signals or barrier semaphores. Data moves between devices by JAX's collectives and lax.ppermute only.
A program may use at most 64 MiB of HBM per device.

```python
import math
import jax
import jax.numpy as jnp
import numpy as np
from jax import lax

D = 2048
FF = 1024
ROWS = 160
EXPERTS = 64
CAP = 7
TOKENS = 10240
N_DP = 8
N_EXPERT = 64


def level_of(key, extent, pieces, least, top_value):
    level, own = 1.0, jax.random.fold_in(key, 6)
    for dim, blocks in pieces:
        steps = jnp.exp(jax.random.uniform(jax.random.fold_in(own, dim), (blocks,), jnp.float32, least / len(pieces), top_value / len(pieces)))
        level = level * jnp.repeat(steps, extent[dim] // blocks).reshape([-1 if axis == dim else 1 for axis in range(len(extent))])
    return level


def deal_out(rng, own, number, rows, amount, top, limit, skew):
    sequence = jax.random.permutation(rng, amount)
    crowded, ordinary = load_shares(amount, rows * top, limit, skew, True), load_shares(amount, rows * top, limit, skew, False)
    places = jnp.arange(amount)

    def named(lengths, rotation):
        used = int((lengths > 0).sum())
        fixed = max(1, used // 4)
        passed = fixed + (places - fixed + rotation * (used - fixed)) % max(1, amount - fixed)
        return jnp.zeros((amount,), jnp.int32).at[sequence[jnp.where(places < fixed, places, passed)]].set(jnp.asarray(lengths, jnp.int32))

    lengths = jnp.where(number % 4 == 0, named(crowded, number // 4), named(ordinary, number - number // 4 - 1))
    mixed = jax.random.permutation(jax.random.fold_in(own, 3), amount)
    donor, receiver = mixed[0:amount // 2 * 2:2], mixed[1:amount // 2 * 2:2]
    slack = jnp.minimum(lengths[donor] - 1, limit - lengths[receiver]) // 2
    slack = jnp.where((donor == sequence[0]) | (receiver == sequence[0]) | (lengths[receiver] == 0), 0, jnp.maximum(slack, 0))
    passed = jax.random.randint(jax.random.fold_in(own, 4), (amount // 2,), 0, 1 << 20) % (slack + 1)
    lengths = lengths.at[donor].add(-passed).at[receiver].add(passed)
    labels = jnp.searchsorted(jnp.cumsum(lengths), jnp.arange(rows * top), side="right").astype(jnp.int32)
    grid = labels.reshape(top, rows).T
    grid = grid[jax.random.permutation(jax.random.fold_in(own, 1), rows)]
    rotation = jax.random.randint(jax.random.fold_in(own, 2), (rows, 1), 0, top)
    return jnp.take_along_axis(grid, (jnp.arange(top)[None, :] + rotation) % top, axis=1)


def load_shares(amount, total, most, lean, full):
    weights = [(1 << 20) // math.isqrt(grade ** lean) + 1 for grade in range(1, amount + 1)]
    largest = most if full else min(most, max(-(-total // amount), total * weights[0] // sum(weights)))
    least = 1 if total - largest >= amount - 1 else 0
    holding, surplus = [largest] + [least] * (amount - 1), total - largest - least * (amount - 1)
    while surplus > 0:
        candidates = [i for i in range(1, amount) if holding[i] < largest] or [i for i in range(1, amount) if holding[i] < most]
        mass, remaining = sum([weights[i] for i in candidates]), surplus
        for i in candidates:
            addition = min(most - holding[i], max(1, remaining * weights[i] // mass), surplus)
            holding[i] = holding[i] + addition
            surplus = surplus - addition
    return np.array(holding)


def scatter_about(stream_key, dims, scale, reach, split=(), held_as=jnp.bfloat16):
    gain = level_of(stream_key, dims, split, -0.22, 0.18) if split else 1.0
    result = jax.random.normal(stream_key, dims, jnp.float32) * scale * gain
    return jnp.minimum(jnp.maximum(result, -reach), reach).astype(held_as)


def setup_inputs(seed: int = 0) -> dict:
    seeds = jax.random.split(jax.random.key(seed), 8)
    tokens = scatter_about(seeds[0], (TOKENS, D), 1.0, 6.0, ((0, 64), (1, 8)))
    grad_out = scatter_about(seeds[1], (TOKENS, D), 1.0, 6.0, ((0, 64), (1, 8)))
    expert_ids_keys = jax.random.split(jax.random.fold_in(seeds[2], 1), TOKENS // ROWS)
    expert_ids_turns = jax.random.permutation(jax.random.fold_in(seeds[2], 3), TOKENS // ROWS)
    expert_ids = jax.vmap(lambda own, number: deal_out(jax.random.fold_in(seeds[2], 2), own, number, ROWS, EXPERTS, 2, CAP, 2))(expert_ids_keys, expert_ids_turns).reshape((TOKENS, 2))
    gate_probs = jnp.clip(jnp.exp(math.log(1.0) - 2.3025851 * jax.random.uniform(seeds[3], (TOKENS, 2), jnp.float32) ** level_of(seeds[3], (TOKENS, 2), ((0, 64),), -0.2, 0.2)), 0.1, 1.0)
    gate_weight = scatter_about(seeds[4], (EXPERTS, D, FF), D ** -0.5, 0.125, ((0, 64), (2, 8)))
    up_weight = scatter_about(seeds[5], (EXPERTS, D, FF), D ** -0.5, 0.125, ((0, 64), (2, 8)))
    down_weight = scatter_about(seeds[6], (EXPERTS, FF, D), FF ** -0.5, 0.1875, ((0, 64), (1, 8)))
    return dict(tokens=tokens, grad_out=grad_out, expert_ids=expert_ids, gate_probs=gate_probs, gate_weight=gate_weight, up_weight=up_weight, down_weight=down_weight)


def reference(tokens, grad_out, expert_ids, gate_probs, gate_weight, up_weight, down_weight):
    blocks = expert_ids.reshape(N_EXPERT, ROWS * 2)
    onehot = (blocks[:, :, None] == jnp.arange(EXPERTS, dtype=jnp.int32)[None, None, :]).astype(jnp.int32)
    before = jnp.cumsum(onehot, axis=1) - onehot
    slot_index = jnp.sum(before * onehot, axis=2).astype(jnp.int32)
    block_index = jnp.broadcast_to(jnp.arange(N_EXPERT, dtype=jnp.int32)[:, None], blocks.shape)
    assign = jnp.arange(N_EXPERT * ROWS * 2, dtype=jnp.int32).reshape(N_EXPERT, ROWS * 2)
    owner_table = jnp.full((EXPERTS, N_EXPERT, CAP), -1, jnp.int32).at[blocks, block_index, slot_index].set(assign)
    flat_probs = gate_probs.reshape(N_EXPERT * ROWS * 2)
    group_width = FF // N_DP
    buffer_rows = N_EXPERT * CAP

    def one_expert(expert):
        owners = owner_table[expert].reshape(buffer_rows)
        is_valid = owners >= 0
        safe_index = jnp.maximum(owners, 0)
        row_index = safe_index // 2
        routed = jnp.where(is_valid[:, None], jnp.take(tokens, row_index, axis=0), jnp.zeros((), tokens.dtype))
        factor = jnp.where(is_valid, jnp.take(flat_probs, safe_index), jnp.zeros((), flat_probs.dtype))
        routed_grad = (jnp.take(grad_out, row_index, axis=0).astype(jnp.float32) * factor[:, None]).astype(jnp.bfloat16)
        gate_mat = gate_weight[expert]
        up_mat = up_weight[expert]
        down_mat = down_weight[expert]
        gate_pre = jnp.dot(routed, gate_mat, preferred_element_type=jnp.float32)
        up_pre = jnp.dot(routed, up_mat, preferred_element_type=jnp.float32)
        sigmoid_gate = jax.nn.sigmoid(gate_pre)
        activated = gate_pre * sigmoid_gate
        hidden = (activated * up_pre).astype(jnp.bfloat16)
        parts = jnp.einsum("rjf,jfd->jrd", hidden.astype(jnp.float32).reshape(buffer_rows, N_DP, group_width), down_mat.astype(jnp.float32).reshape(N_DP, group_width, D)).astype(jnp.bfloat16)
        expert_out = jnp.sum(parts.astype(jnp.float32), axis=0)
        grad_hidden = jnp.dot(routed_grad, down_mat.T, preferred_element_type=jnp.float32)
        grad_gate_pre = (grad_hidden * up_pre * sigmoid_gate * (1.0 + gate_pre * (1.0 - sigmoid_gate))).astype(jnp.bfloat16)
        grad_up_pre = (grad_hidden * activated).astype(jnp.bfloat16)
        grad_down = jnp.dot(hidden.T, routed_grad, preferred_element_type=jnp.float32).astype(jnp.bfloat16)
        grad_gate = jnp.dot(routed.T, grad_gate_pre, preferred_element_type=jnp.float32).astype(jnp.bfloat16)
        grad_up = jnp.dot(routed.T, grad_up_pre, preferred_element_type=jnp.float32).astype(jnp.bfloat16)
        backs = jnp.einsum("rjf,djf->jrd", grad_gate_pre.astype(jnp.float32).reshape(buffer_rows, N_DP, group_width), gate_mat.astype(jnp.float32).reshape(D, N_DP, group_width))
        backs = backs + jnp.einsum("rjf,djf->jrd", grad_up_pre.astype(jnp.float32).reshape(buffer_rows, N_DP, group_width), up_mat.astype(jnp.float32).reshape(D, N_DP, group_width))
        expert_back = jnp.sum(backs.astype(jnp.bfloat16).astype(jnp.float32), axis=0)
        return expert_out, expert_back, grad_gate, grad_up, grad_down

    expert_out, expert_back, grad_gate_weight, grad_up_weight, grad_down_weight = lax.map(one_expert, jnp.arange(EXPERTS, dtype=jnp.int32))
    gather_index = (blocks * buffer_rows + block_index * CAP + slot_index).reshape(N_EXPERT * ROWS * 2).astype(jnp.int32)
    out_rows = jnp.take(expert_out.reshape(EXPERTS * buffer_rows, D), gather_index, axis=0) * flat_probs[:, None]
    layer_out = out_rows.reshape(TOKENS, 2, D).sum(axis=1).astype(jnp.bfloat16)
    back_rows = jnp.take(expert_back.reshape(EXPERTS * buffer_rows, D), gather_index, axis=0)
    grad_tokens = back_rows.reshape(TOKENS, 2, D).sum(axis=1).astype(jnp.bfloat16)
    return layer_out, grad_tokens, grad_gate_weight, grad_up_weight, grad_down_weight
```

```python
import functools

import jax
import jax.numpy as jnp
from jax import lax
from jax.experimental import pallas as pl
from jax.experimental.pallas import tpu as pltpu
from jax.sharding import PartitionSpec as P

BF16, F32, I32 = jnp.bfloat16, jnp.float32, jnp.int32
PAD = 8


def dot(a, b, ca=1, cb=0):
    return lax.dot_general(a, b, (((ca,), (cb,)), ((), ())), preferred_element_type=F32)


def call(body, outs, args, flops, in_specs=None):
    moved = sum(a.size * a.dtype.itemsize for a in args)
    moved += sum(o.size * o.dtype.itemsize for o in outs)
    vmem = pl.BlockSpec(memory_space=pltpu.VMEM)
    return pl.pallas_call(
        body,
        out_shape=outs,
        in_specs=in_specs or [vmem] * len(args),
        out_specs=[vmem] * len(outs),
        cost_estimate=pl.CostEstimate(flops=flops, bytes_accessed=moved, transcendentals=0),
    )(*args)


def iota(shape, dim):
    return lax.broadcasted_iota(I32, shape, dim)


def route_body(experts, capacity, ids_ref, probs_ref, tok_ref, grad_ref, out_ref, pos_ref):
    ids, probs = ids_ref[...], probs_ref[...]
    rows = ids.shape[1]
    width = tok_ref.shape[1]
    named = [iota((experts, rows), 0) == ids[k : k + 1, :] for k in range(2)]
    both = (named[0].astype(F32) + named[1].astype(F32)).astype(BF16)
    earlier = (iota((rows, rows), 0) < iota((rows, rows), 1)).astype(F32).astype(BF16)
    before = dot(both, earlier)
    place = iota((experts * PAD, rows), 0)
    here = []
    for k in range(2):
        slot = jnp.sum(jnp.where(named[k], before, 0.0), axis=0, keepdims=True).astype(I32)
        pos_ref[k : k + 1, :] = ids[k : k + 1, :] * capacity + slot
        here.append(place == ids[k : k + 1, :] * PAD + slot)
    picks = (here[0] | here[1]).astype(F32).astype(BF16)
    factor = jnp.sum(
        jnp.where(here[0], probs[0:1, :], jnp.where(here[1], probs[1:2, :], 0.0)),
        axis=1,
        keepdims=True,
    )
    out_ref[:, :width] = dot(picks, tok_ref[...]).astype(BF16)
    out_ref[:, width:] = (dot(picks, grad_ref[...]) * factor).astype(BF16)


def combine_body(pos_ref, probs_ref, back_ref, out_ref, grad_ref):
    pos, probs = pos_ref[...], probs_ref[...]
    rows = pos.shape[1]
    width = out_ref.shape[1]
    returned = back_ref[...]
    place = iota((returned.shape[0], rows), 0)
    rows_of = [
        dot((place == pos[k : k + 1, :]).astype(F32).astype(BF16), returned, 0, 0)
        for k in range(2)
    ]
    out_ref[...] = (
        rows_of[0][:, :width] * probs[:, 0:1] + rows_of[1][:, :width] * probs[:, 1:2]
    ).astype(BF16)
    grad_ref[...] = (rows_of[0][:, width:] + rows_of[1][:, width:]).astype(BF16)


def block_of(me_ref, mask, width):
    return pl.ds(pl.multiple_of((me_ref[0] ^ mask) * width, width), width)


def partial_pre(me_ref, mask, x, gate_ref, up_ref, down_ref):
    width = x.shape[1] // 2
    at = block_of(me_ref, mask, width)
    both = jnp.concatenate([gate_ref[at, :], up_ref[at, :]], axis=1)
    return dot(x[:, :width], both), dot(x[:, width:], down_ref[:, at], 1, 1)


def first_body(masks, me_ref, *refs):
    xs, (gate_ref, up_ref, down_ref, pre_ref, hid_ref) = refs[: len(masks)], refs[len(masks) :]
    pre, hid = 0.0, 0.0
    for mask, x_ref in zip(masks, xs):
        a, b = partial_pre(me_ref, mask, x_ref[...], gate_ref, up_ref, down_ref)
        pre, hid = pre + a, hid + b
    pre_ref[...] = pre
    hid_ref[...] = hid


def shares(me_ref, mask, width, hidden, pre_grads, gate_ref, up_ref, down_ref, out_ref, row):
    at = block_of(me_ref, mask, width)
    rows = pl.ds(row, hidden.shape[0])
    out_ref[rows, :width] = dot(hidden, down_ref[:, at]).astype(BF16)
    both = jnp.concatenate([gate_ref[at, :], up_ref[at, :]], axis=1)
    out_ref[rows, width:] = dot(pre_grads, both, 1, 1).astype(BF16)


def second_body(masks, me_ref, *refs):
    xs, rest = refs[: len(masks)], refs[len(masks) :]
    pre_ref, hid_ref, gate_ref, up_ref, down_ref, h_ref, g_ref, near_ref, far_ref = rest
    pre, hid = pre_ref[...], hid_ref[...]
    for mask, x_ref in zip(masks, xs):
        a, b = partial_pre(me_ref, mask, x_ref[...], gate_ref, up_ref, down_ref)
        pre, hid = pre + a, hid + b
    units = hid.shape[1]
    gate, up = pre[:, :units], pre[:, units:]
    sig = jax.nn.sigmoid(gate)
    silu = gate * sig
    hidden = (silu * up).astype(BF16)
    gate_grad = (hid * up * sig * (1.0 + gate * (1.0 - sig))).astype(BF16)
    up_grad = (hid * silu).astype(BF16)
    grads = jnp.concatenate([gate_grad, up_grad], axis=1)
    h_ref[...] = hidden
    g_ref[...] = grads
    width = near_ref.shape[1] // 2
    n = hidden.shape[0]
    shares(me_ref, 5, width, hidden, grads, gate_ref, up_ref, down_ref, near_ref, 0)
    for i, mask in enumerate((7, 3, 1)):
        shares(me_ref, mask, width, hidden, grads, gate_ref, up_ref, down_ref, far_ref, i * n)


def third_body(me_ref, h_ref, g_ref, gate_ref, up_ref, down_ref, own_ref):
    width = own_ref.shape[1] // 2
    hidden, grads = h_ref[...], g_ref[...]
    n = hidden.shape[0]
    for i, mask in enumerate((4, 6, 2, 0)):
        shares(me_ref, mask, width, hidden, grads, gate_ref, up_ref, down_ref, own_ref, i * n)


def weight_grads_body(masks, me_ref, *refs):
    xs, (h_ref, g_ref, gate_out, up_out, down_out) = refs[: len(masks)], refs[len(masks) :]
    hidden, grads = h_ref[...], g_ref[...]
    units = hidden.shape[1]
    for mask, x_ref in zip(masks, xs):
        x = x_ref[...]
        width = x.shape[1] // 2
        at = block_of(me_ref, mask, width)
        both = dot(x[:, :width], grads, 0, 0)
        gate_out[at, :] = both[:, :units].astype(BF16)
        up_out[at, :] = both[:, units:].astype(BF16)
        down_out[:, at] = dot(hidden, x[:, width:], 0, 0).astype(BF16)


def per_device(tokens, grad_out, expert_ids, gate_probs, gate_weight, up_weight, down_weight):
    experts, parts = lax.axis_size("expert"), lax.axis_size("dp")
    rows, width = tokens.shape
    capacity = max(2, 3 * rows // experts)
    n = experts * capacity
    gate, up, down = gate_weight[0], up_weight[0], down_weight[0]
    units, model = down.shape
    me = lax.axis_index("dp").astype(I32).reshape(1)
    sds = jax.ShapeDtypeStruct

    def swap(x, mask):
        return lax.ppermute(x, "dp", [(j, j ^ mask) for j in range(parts)])

    smem, vmem = pl.BlockSpec(memory_space=pltpu.SMEM), pl.BlockSpec(memory_space=pltpu.VMEM)

    send, pos = call(
        functools.partial(route_body, experts, capacity),
        [sds((experts * PAD, 2 * width), BF16), sds((2, rows), I32)],
        [expert_ids.T, gate_probs.T, tokens, grad_out],
        4 * experts * PAD * rows * width,
    )
    filled = lax.all_to_all(
        send.reshape(experts, PAD, 2 * width), "expert", split_axis=0, concat_axis=0, tiled=True
    )
    x = {0: filled[:, :capacity].reshape(n, 2 * width)}
    x[6] = swap(x[0], 6)
    x[2] = swap(x[0], 2)
    x[1] = swap(x[0], 1)
    x[4] = swap(x[6], 2)
    x[7] = swap(x[6], 1)
    x[3] = swap(x[2], 1)
    x[5] = swap(x[4], 1)

    weights = [gate, up, down]
    early, late = (0, 1, 2, 3, 6, 7), (4, 5)
    per_mask = 6 * n * width * units
    pre, hid = call(
        functools.partial(first_body, early),
        [sds((n, 2 * units), F32), sds((n, units), F32)],
        [me, *[x[m] for m in early], *weights],
        len(early) * per_mask,
        [smem] + [vmem] * (len(early) + 3),
    )
    hidden, grads, near, far = call(
        functools.partial(second_body, late),
        [
            sds((n, units), BF16),
            sds((n, 2 * units), BF16),
            sds((n, 2 * width), BF16),
            sds((3 * n, 2 * width), BF16),
        ],
        [me, *[x[m] for m in late], pre, hid, *weights],
        (len(late) + 4) * per_mask,
        [smem] + [vmem] * (len(late) + 5),
    )
    near_in = swap(near, 1)
    far_in = swap(far, 1)
    (own,) = call(
        third_body,
        [sds((4 * n, 2 * width), BF16)],
        [me, hidden, grads, *weights],
        4 * per_mask,
        [smem] + [vmem] * 5,
    )

    def own_of(i):
        return own[i * n : (i + 1) * n].astype(F32)

    def far_of(i):
        return far_in[i * n : (i + 1) * n].astype(F32)

    across = swap((own_of(0) + near_in.astype(F32)).astype(BF16), 2)
    side = swap((own_of(2) + far_of(1)).astype(BF16), 2)
    over = swap((own_of(1) + far_of(0) + across.astype(F32)).astype(BF16), 6)
    total = own_of(3) + far_of(2) + side.astype(F32) + over.astype(F32)

    gate_grad, up_grad, down_grad = call(
        functools.partial(weight_grads_body, tuple(range(parts))),
        [sds((model, units), BF16), sds((model, units), BF16), sds((units, model), BF16)],
        [me, *[x[m] for m in range(parts)], hidden, grads],
        parts * per_mask,
        [smem] + [vmem] * (parts + 2),
    )

    returned = lax.all_to_all(
        total.astype(BF16).reshape(experts, capacity, 2 * width),
        "expert",
        split_axis=0,
        concat_axis=0,
        tiled=True,
    ).reshape(n, 2 * width)
    layer_out, grad_tokens = call(
        combine_body,
        [sds((rows, width), BF16), sds((rows, width), BF16)],
        [pos, gate_probs, returned],
        8 * n * rows * width,
    )
    return layer_out, grad_tokens, gate_grad[None], up_grad[None], down_grad[None]


def solution(mesh):
    return jax.shard_map(
        per_device,
        mesh=mesh,
        in_specs=(
            P("expert", "dp"),
            P("expert", "dp"),
            P("expert", None),
            P("expert", None),
            P("expert", None, "dp"),
            P("expert", None, "dp"),
            P("expert", "dp", None),
        ),
        out_specs=(
            P("expert", "dp"),
            P("expert", "dp"),
            P("expert", None, "dp"),
            P("expert", None, "dp"),
            P("expert", "dp", None),
        ),
        check_vma=False,
    )
```

```python
import functools

import jax
import jax.numpy as jnp
from jax import lax
from jax.experimental import pallas as pl
from jax.experimental.pallas import tpu as pltpu
from jax.sharding import Mesh
from jax.sharding import PartitionSpec as P

BF16, F32, I32 = jnp.bfloat16, jnp.float32, jnp.int32
PAD = 8
DP = ("za", "zb", "core")
FAR, CHIP, CORE = 4, 2, 1
FEATURES = (0, FAR)
QUAD = (0, CORE, CHIP, CORE + CHIP)


def dot(a, b, ca=1, cb=0):
    return lax.dot_general(a, b, (((ca,), (cb,)), ((), ())), preferred_element_type=F32)


def call(body, outs, args, flops, me=None):
    moved = sum(a.size * a.dtype.itemsize for a in args)
    moved += sum(o.size * o.dtype.itemsize for o in outs)
    vmem, smem = pl.BlockSpec(memory_space=pltpu.VMEM), pl.BlockSpec(memory_space=pltpu.SMEM)
    head = [] if me is None else [me]
    return pl.pallas_call(
        body,
        out_shape=outs,
        in_specs=[smem] * len(head) + [vmem] * len(args),
        out_specs=[vmem] * len(outs),
        cost_estimate=pl.CostEstimate(flops=flops, bytes_accessed=moved, transcendentals=0),
    )(*head, *args)


def iota(shape, dim):
    return lax.broadcasted_iota(I32, shape, dim)


def route_body(experts, capacity, ids_ref, probs_ref, tok_ref, grad_ref, out_ref, pos_ref):
    ids, probs = ids_ref[...], probs_ref[...]
    rows = ids.shape[1]
    width = tok_ref.shape[1]
    named = [iota((experts, rows), 0) == ids[k : k + 1, :] for k in range(2)]
    both = (named[0].astype(F32) + named[1].astype(F32)).astype(BF16)
    earlier = (iota((rows, rows), 0) < iota((rows, rows), 1)).astype(F32).astype(BF16)
    before = dot(both, earlier)
    place = iota((experts * PAD, rows), 0)
    here = []
    for k in range(2):
        slot = jnp.sum(jnp.where(named[k], before, 0.0), axis=0, keepdims=True).astype(I32)
        pos_ref[k : k + 1, :] = ids[k : k + 1, :] * capacity + slot
        here.append(place == ids[k : k + 1, :] * PAD + slot)
    picks = (here[0] | here[1]).astype(F32).astype(BF16)
    factor = jnp.sum(
        jnp.where(here[0], probs[0:1, :], jnp.where(here[1], probs[1:2, :], 0.0)),
        axis=1,
        keepdims=True,
    )
    routed = dot(picks, tok_ref[...]).astype(BF16)
    routed_grad = (dot(picks, grad_ref[...]) * factor).astype(BF16)
    for i in range(len(FEATURES)):
        at = pl.ds(i * experts * PAD, experts * PAD)
        out_ref[at, :width] = routed
        out_ref[at, width:] = routed_grad


def combine_body(pos_ref, probs_ref, back_ref, out_ref, grad_ref):
    pos, probs = pos_ref[...], probs_ref[...]
    rows = pos.shape[1]
    width = out_ref.shape[1]
    n = back_ref.shape[0] // len(FEATURES)
    place = iota((n, rows), 0)
    sums = []
    for k in range(2):
        pick = (place == pos[k : k + 1, :]).astype(F32).astype(BF16)
        sums.append(
            sum(dot(pick, back_ref[pl.ds(i * n, n), :], 0, 0) for i in range(len(FEATURES)))
        )
    out_ref[...] = (sums[0][:, :width] * probs[:, 0:1] + sums[1][:, :width] * probs[:, 1:2]).astype(
        BF16
    )
    grad_ref[...] = (sums[0][:, width:] + sums[1][:, width:]).astype(BF16)


def block_of(me_ref, mask, width):
    return pl.ds(pl.multiple_of((me_ref[0] ^ mask) * width, width), width)


def half_of(me_ref, i, n):
    far = jnp.where((me_ref[0] & FAR) == 0, i, 1 - i)
    return pl.ds(pl.multiple_of(far * n, n), n)


def pack_body(me_ref, gate_ref, up_ref, down_ref, *out_refs):
    width = out_refs[0].shape[0] // len(FEATURES)
    units = gate_ref.shape[1]
    for h, out_ref in zip(QUAD, out_refs):
        for i, f in enumerate(FEATURES):
            at, to = block_of(me_ref, h ^ f, width), pl.ds(i * width, width)
            out_ref[to, :units] = gate_ref[at, :]
            out_ref[to, units : 2 * units] = up_ref[at, :]
            out_ref[to, 2 * units :] = down_ref[:, at].T


def pre_body(me_ref, x_ref, first_ref, second_ref, *out_refs):
    n = x_ref.shape[0] // len(FEATURES)
    width = x_ref.shape[1] // 2
    units = first_ref.shape[1] // 3
    pres, hids = [0.0, 0.0], 0.0
    for i in range(len(FEATURES)):
        rows, w = half_of(me_ref, i, n), pl.ds(i * width, width)
        x, g = x_ref[rows, :width], x_ref[rows, width:]
        for j, ref in enumerate((first_ref, second_ref)):
            pres[j] = pres[j] + dot(x, ref[w, : 2 * units])
        downs = jnp.concatenate([first_ref[w, 2 * units :], second_ref[w, 2 * units :]], axis=1)
        hids = hids + dot(g, downs)
    for j, ref in enumerate(out_refs):
        ref[:, : 2 * units] = pres[j].astype(ref.dtype)
        ref[:, 2 * units :] = hids[:, j * units : (j + 1) * units].astype(ref.dtype)


def act_body(keep_ref, core_ref, chip_ref, out_ref):
    units = keep_ref.shape[1] // 3
    pre = keep_ref[...] + core_ref[...].astype(F32) + chip_ref[...].astype(F32)
    gate, up, hid = pre[:, :units], pre[:, units : 2 * units], pre[:, 2 * units :]
    sig = jax.nn.sigmoid(gate)
    silu = gate * sig
    out_ref[:, :units] = (silu * up).astype(BF16)
    out_ref[:, units : 2 * units] = (hid * up * sig * (1.0 + gate * (1.0 - sig))).astype(BF16)
    out_ref[:, 2 * units :] = (hid * silu).astype(BF16)


def result_body(first, me_ref, *refs):
    h_refs, w_refs = refs[:2], refs[2:4]
    acc_ref, out_ref = (None, refs[4]) if first else (refs[4], refs[5])
    n = h_refs[0].shape[0]
    units = h_refs[0].shape[1] // 3
    width = w_refs[0].shape[0] // len(FEATURES)
    hidden = jnp.concatenate([h[:, :units] for h in h_refs], axis=1)
    grads = jnp.concatenate([h[:, units:] for h in h_refs], axis=1)
    for i in range(len(FEATURES)):
        w = pl.ds(i * width, width)
        downs = jnp.concatenate([r[w, 2 * units :] for r in w_refs], axis=1)
        pairs = jnp.concatenate([r[w, : 2 * units] for r in w_refs], axis=1)
        out, back = dot(hidden, downs, 1, 1), dot(grads, pairs, 1, 1)
        if first:
            rows = pl.ds(i * n, n)
            out_ref[rows, :width] = out
            out_ref[rows, width:] = back
        else:
            rows, held = half_of(me_ref, i, n), pl.ds(i * n, n)
            out_ref[rows, :width] = (out + acc_ref[held, :width]).astype(BF16)
            out_ref[rows, width:] = (back + acc_ref[held, width:]).astype(BF16)


def weight_grads_body(me_ref, x_ref, *refs):
    h_refs, out_refs = refs[: len(QUAD)], refs[len(QUAD) :]
    n = x_ref.shape[0] // len(FEATURES)
    width = x_ref.shape[1] // 2
    units = h_refs[0].shape[1] // 3
    for i in range(len(FEATURES)):
        rows, to = half_of(me_ref, i, n), pl.ds(i * width, width)
        x, g = x_ref[rows, :width], x_ref[rows, width:]
        for h_ref, out_ref in zip(h_refs, out_refs):
            out_ref[to, : 2 * units] = dot(x, h_ref[:, units:], 0, 0).astype(BF16)
            out_ref[to, 2 * units :] = dot(g, h_ref[:, :units], 0, 0).astype(BF16)


def merge_body(me_ref, *refs):
    in_refs, (gate_ref, up_ref, down_ref) = refs[: len(QUAD)], refs[len(QUAD) :]
    width = in_refs[0].shape[0] // len(FEATURES)
    units = gate_ref.shape[1]
    for h, ref in zip(QUAD, in_refs):
        for i, f in enumerate(FEATURES):
            at, w = block_of(me_ref, h ^ f, width), pl.ds(i * width, width)
            gate_ref[at, :] = ref[w, :units]
            up_ref[at, :] = ref[w, units : 2 * units]
            down_ref[:, at] = ref[w, 2 * units :].T


def per_device(tokens, grad_out, expert_ids, gate_probs, gate_weight, up_weight, down_weight):
    experts = lax.axis_size("expert")
    rows, width = tokens.shape
    capacity = max(2, 3 * rows // experts)
    n, copies, quad = experts * capacity, len(FEATURES), len(QUAD)
    gate, up, down = gate_weight[0], up_weight[0], down_weight[0]
    units, model = down.shape
    me = lax.axis_index(DP).astype(I32).reshape(1)
    sds = jax.ShapeDtypeStruct
    per_pair = 6 * n * width * units

    def swap(x, mask):
        return lax.ppermute(x, DP, [(j, j ^ mask) for j in range(8)])

    send, pos = call(
        functools.partial(route_body, experts, capacity),
        [sds((copies * experts * PAD, 2 * width), BF16), sds((2, rows), I32)],
        [expert_ids.T, gate_probs.T, tokens, grad_out],
        4 * experts * PAD * rows * width,
    )
    filled = lax.all_to_all(
        send.reshape(copies * experts, PAD, 2 * width),
        ("za", "expert"),
        split_axis=0,
        concat_axis=0,
        tiled=True,
    )
    packs = call(
        pack_body,
        [sds((copies * width, 3 * units), BF16)] * quad,
        [gate, up, down],
        0,
        me,
    )
    w = [p if h == 0 else swap(p, h) for h, p in zip(QUAD, packs)]
    filled, *w = lax.optimization_barrier((filled, *w))
    x = filled[:, :capacity].reshape(copies * n, 2 * width)

    core_out = call(
        pre_body,
        [sds((n, 3 * units), BF16)] * 2,
        [x, w[1], w[3]],
        2 * copies * per_pair,
        me,
    )
    core_in = swap(jnp.concatenate(core_out, axis=0), CORE)
    keep = call(
        pre_body,
        [sds((n, 3 * units), F32)] * 2,
        [x, w[0], w[2]],
        2 * copies * per_pair,
        me,
    )
    chip_in = swap((keep[1] + core_in[n:].astype(F32)).astype(BF16), CHIP)
    (h0,) = call(
        act_body, [sds((n, 3 * units), BF16)], [keep[0], core_in[:n], chip_in], 0
    )
    h2 = swap(h0, CHIP)
    h1 = swap(h0, CORE)
    (acc,) = call(
        functools.partial(result_body, True),
        [sds((copies * n, 2 * width), F32)],
        [h0, h1, w[0], w[1]],
        2 * copies * per_pair,
        me,
    )
    h3 = swap(h2, CORE)
    (result,) = call(
        functools.partial(result_body, False),
        [sds((copies * n, 2 * width), BF16)],
        [h2, h3, w[2], w[3], acc],
        2 * copies * per_pair,
        me,
    )
    returned = lax.all_to_all(
        result.reshape(copies * experts, capacity, 2 * width),
        ("za", "expert"),
        split_axis=0,
        concat_axis=0,
        tiled=True,
    )
    shares = call(
        weight_grads_body,
        [sds((copies * width, 3 * units), BF16)] * quad,
        [x, h0, h1, h2, h3],
        quad * copies * per_pair,
        me,
    )
    got = [s if h == 0 else swap(s, h) for h, s in zip(QUAD, shares)]
    gate_grad, up_grad, down_grad = call(
        merge_body,
        [sds((model, units), BF16), sds((model, units), BF16), sds((units, model), BF16)],
        got,
        0,
        me,
    )
    layer_out, grad_tokens = call(
        combine_body,
        [sds((rows, width), BF16), sds((rows, width), BF16)],
        [pos, gate_probs, returned.reshape(copies * n, 2 * width)],
        8 * copies * n * rows * width,
    )
    return layer_out, grad_tokens, gate_grad[None], up_grad[None], down_grad[None]


def solution(mesh):
    experts = mesh.shape["expert"]
    fine = Mesh(mesh.devices.reshape(2, 2, 2, experts), (*DP, "expert"))
    return jax.shard_map(
        per_device,
        mesh=fine,
        in_specs=(
            P("expert", DP),
            P("expert", DP),
            P("expert", None),
            P("expert", None),
            P("expert", None, DP),
            P("expert", None, DP),
            P("expert", DP, None),
        ),
        out_specs=(
            P("expert", DP),
            P("expert", DP),
            P("expert", None, DP),
            P("expert", None, DP),
            P("expert", DP, None),
        ),
        check_vma=False,
    )
```

```python
import functools

import jax
import jax.numpy as jnp
from jax import lax
from jax.experimental import pallas as pl
from jax.experimental.pallas import tpu as pltpu
from jax.sharding import Mesh
from jax.sharding import PartitionSpec as P


BF16, F32, I32 = jnp.bfloat16, jnp.float32, jnp.int32
PAD = 8
DP = ("za", "zb", "core")
FAR, CHIP, CORE = 4, 2, 1
FEATURES = (0, FAR)


def dot(a, b, ca=1, cb=0):
    return lax.dot_general(a, b, (((ca,), (cb,)), ((), ())), preferred_element_type=F32)


def call(body, outs, args, flops, me=None):
    moved = sum(a.size * a.dtype.itemsize for a in args)
    moved += sum(o.size * o.dtype.itemsize for o in outs)
    vmem, smem = pl.BlockSpec(memory_space=pltpu.VMEM), pl.BlockSpec(memory_space=pltpu.SMEM)
    head = [] if me is None else [me]
    return pl.pallas_call(
        body,
        out_shape=outs,
        in_specs=[smem] * len(head) + [vmem] * len(args),
        out_specs=[vmem] * len(outs),
        cost_estimate=pl.CostEstimate(flops=flops, bytes_accessed=moved, transcendentals=0),
    )(*head, *args)


def iota(shape, dim):
    return lax.broadcasted_iota(I32, shape, dim)


def route_body(experts, capacity, ids_ref, probs_ref, tok_ref, grad_ref, out_ref, pos_ref):
    ids, probs = ids_ref[...], probs_ref[...]
    rows = ids.shape[1]
    width = tok_ref.shape[1]
    named = [iota((experts, rows), 0) == ids[k : k + 1, :] for k in range(2)]
    both = (named[0].astype(F32) + named[1].astype(F32)).astype(BF16)
    earlier = (iota((rows, rows), 0) < iota((rows, rows), 1)).astype(F32).astype(BF16)
    before = dot(both, earlier)
    place = iota((experts * PAD, rows), 0)
    here = []
    for k in range(2):
        slot = jnp.sum(jnp.where(named[k], before, 0.0), axis=0, keepdims=True).astype(I32)
        pos_ref[k : k + 1, :] = ids[k : k + 1, :] * capacity + slot
        here.append(place == ids[k : k + 1, :] * PAD + slot)
    picks = (here[0] | here[1]).astype(F32).astype(BF16)
    factor = jnp.sum(
        jnp.where(here[0], probs[0:1, :], jnp.where(here[1], probs[1:2, :], 0.0)),
        axis=1,
        keepdims=True,
    )
    routed = dot(picks, tok_ref[...]).astype(BF16)
    routed_grad = (dot(picks, grad_ref[...]) * factor).astype(BF16)
    for i in range(len(FEATURES)):
        at = pl.ds(i * experts * PAD, experts * PAD)
        out_ref[at, :width] = routed
        out_ref[at, width:] = routed_grad


def combine_body(pos_ref, probs_ref, back_ref, out_ref, grad_ref):
    pos, probs = pos_ref[...], probs_ref[...]
    rows = pos.shape[1]
    width = out_ref.shape[1]
    n = back_ref.shape[0] // len(FEATURES)
    place = iota((n, rows), 0)
    sums = []
    for k in range(2):
        pick = (place == pos[k : k + 1, :]).astype(F32).astype(BF16)
        sums.append(
            sum(dot(pick, back_ref[pl.ds(i * n, n), :], 0, 0) for i in range(len(FEATURES)))
        )
    out_ref[...] = (sums[0][:, :width] * probs[:, 0:1] + sums[1][:, :width] * probs[:, 1:2]).astype(
        BF16
    )
    grad_ref[...] = (sums[0][:, width:] + sums[1][:, width:]).astype(BF16)


def block_of(me_ref, mask, width):
    return pl.ds(pl.multiple_of((me_ref[0] ^ mask) * width, width), width)


def half_of(me_ref, i, n):
    far = jnp.where((me_ref[0] & FAR) == 0, i, 1 - i)
    return pl.ds(pl.multiple_of(far * n, n), n)


def pack_body(masks, me_ref, gate_ref, up_ref, down_ref, out_ref):
    width = out_ref.shape[0] // len(masks)
    units = gate_ref.shape[1]
    for i, mask in enumerate(masks):
        at, to = block_of(me_ref, mask, width), pl.ds(i * width, width)
        out_ref[to, :units] = gate_ref[at, :]
        out_ref[to, units : 2 * units] = up_ref[at, :]
        out_ref[to, 2 * units :] = down_ref[:, at].T


def pre_body(me_ref, x_ref, first_ref, second_ref, *out_refs):
    n = x_ref.shape[0] // len(FEATURES)
    width = x_ref.shape[1] // 2
    units = first_ref.shape[1] // 3
    pres, hids = [0.0, 0.0], 0.0
    for i in range(len(FEATURES)):
        rows, w = half_of(me_ref, i, n), pl.ds(i * width, width)
        x, g = x_ref[rows, :width], x_ref[rows, width:]
        for j, ref in enumerate((first_ref, second_ref)):
            pres[j] = pres[j] + dot(x, ref[w, : 2 * units])
        downs = jnp.concatenate([first_ref[w, 2 * units :], second_ref[w, 2 * units :]], axis=1)
        hids = hids + dot(g, downs)
    for j, ref in enumerate(out_refs):
        ref[:, : 2 * units] = pres[j].astype(ref.dtype)
        ref[:, 2 * units :] = hids[:, j * units : (j + 1) * units].astype(ref.dtype)


def act_body(keep_ref, core_ref, chip_ref, out_ref):
    units = keep_ref.shape[1] // 3
    pre = keep_ref[...] + core_ref[...].astype(F32) + chip_ref[...].astype(F32)
    gate, up, hid = pre[:, :units], pre[:, units : 2 * units], pre[:, 2 * units :]
    sig = jax.nn.sigmoid(gate)
    silu = gate * sig
    out_ref[:, :units] = (silu * up).astype(BF16)
    out_ref[:, units : 2 * units] = (hid * up * sig * (1.0 + gate * (1.0 - sig))).astype(BF16)
    out_ref[:, 2 * units :] = (hid * silu).astype(BF16)


def result_body(first, me_ref, *refs):
    h_refs, w_refs = refs[:2], refs[2:4]
    acc_ref, out_ref = (None, refs[4]) if first else (refs[4], refs[5])
    n = h_refs[0].shape[0]
    units = h_refs[0].shape[1] // 3
    width = w_refs[0].shape[0] // len(FEATURES)
    hidden = jnp.concatenate([h[:, :units] for h in h_refs], axis=1)
    grads = jnp.concatenate([h[:, units:] for h in h_refs], axis=1)
    for i in range(len(FEATURES)):
        w = pl.ds(i * width, width)
        downs = jnp.concatenate([r[w, 2 * units :] for r in w_refs], axis=1)
        pairs = jnp.concatenate([r[w, : 2 * units] for r in w_refs], axis=1)
        out, back = dot(hidden, downs, 1, 1), dot(grads, pairs, 1, 1)
        if first:
            rows = pl.ds(i * n, n)
            out_ref[rows, :width] = out
            out_ref[rows, width:] = back
        else:
            rows, held = half_of(me_ref, i, n), pl.ds(i * n, n)
            out_ref[rows, :width] = (out + acc_ref[held, :width]).astype(BF16)
            out_ref[rows, width:] = (back + acc_ref[held, width:]).astype(BF16)


def weight_grads_body(me_ref, own_ref, near_ref, far_ref, h0_ref, h1_ref, keep_ref, send_ref):
    n = near_ref.shape[0]
    width = own_ref.shape[1] // 2
    units = h0_ref.shape[1] // 3
    grads = jnp.concatenate([h0_ref[:, units:], h1_ref[:, units:]], axis=1)
    hidden = jnp.concatenate([h0_ref[:, :units], h1_ref[:, :units]], axis=1)

    def work(x, g, to):
        both, down = dot(x, grads, 0, 0).astype(BF16), dot(g, hidden, 0, 0).astype(BF16)
        keep_ref[to, : 2 * units], send_ref[to, : 2 * units] = both[:, : 2 * units], both[:, 2 * units :]
        keep_ref[to, 2 * units :], send_ref[to, 2 * units :] = down[:, :units], down[:, units:]

    for i in range(len(FEATURES)):
        rows = pl.ds(i * n, n)
        work(own_ref[rows, :width], own_ref[rows, width:], pl.ds(i * width, width))
    for i, ref in enumerate((near_ref, far_ref)):
        at = pl.ds((len(FEATURES) + i) * width, width)
        work(ref[:, :width], ref[:, width:], at)


def merge_body(me_ref, keep_ref, got_ref, gate_ref, up_ref, down_ref):
    units = gate_ref.shape[1]
    width = keep_ref.shape[0] // 4
    for core, ref in ((0, keep_ref), (CORE, got_ref)):
        for i in range(4):
            block = ((me_ref[0] ^ core ^ (CHIP if i >= 2 else 0)) & (FAR - 1)) + FAR * (i % 2)
            at = pl.ds(pl.multiple_of(block * width, width), width)
            w = pl.ds(i * width, width)
            gate_ref[at, :] = ref[w, :units]
            up_ref[at, :] = ref[w, units : 2 * units]
            down_ref[:, at] = ref[w, 2 * units :].T


def per_device(tokens, grad_out, expert_ids, gate_probs, gate_weight, up_weight, down_weight):
    experts = lax.axis_size("expert")
    rows, width = tokens.shape
    capacity = max(2, 3 * rows // experts)
    n, copies = experts * capacity, len(FEATURES)
    gate, up, down = gate_weight[0], up_weight[0], down_weight[0]
    units, model = down.shape
    me = lax.axis_index(DP).astype(I32).reshape(1)
    sds = jax.ShapeDtypeStruct
    per_pair = 6 * n * width * units

    def swap(x, mask):
        return lax.ppermute(x, DP, [(j, j ^ mask) for j in range(8)])

    def pack(*masks):
        return call(
            functools.partial(pack_body, masks),
            [sds((len(masks) * width, 3 * units), BF16)],
            [gate, up, down],
            0,
            me,
        )[0]

    def pre(weights, dtype):
        return call(
            pre_body, [sds((n, 3 * units), dtype)] * 2, [x, *weights], 2 * copies * per_pair, me
        )

    def there_and_back(a):
        return lax.all_to_all(a, ("za", "expert"), split_axis=0, concat_axis=0, tiled=True)

    cut = copies * width
    chip_w = swap(pack(CHIP, CHIP ^ FAR, CHIP ^ CORE, CHIP ^ CORE ^ FAR), CHIP)
    send, pos = call(
        functools.partial(route_body, experts, capacity),
        [sds((copies * experts * PAD, 2 * width), BF16), sds((2, rows), I32)],
        [expert_ids.T, gate_probs.T, tokens, grad_out],
        4 * experts * PAD * rows * width,
    )
    filled = there_and_back(send.reshape(copies * experts, PAD, 2 * width))
    near = pack(0, FAR, CORE, CORE ^ FAR)
    core_w = swap(near[cut:], CORE)
    relay_w = swap(chip_w[cut:], CORE)
    filled, near, core_w, chip_w, relay_w = lax.optimization_barrier(
        (filled, near, core_w, chip_w, relay_w)
    )
    w = {0: near[:cut], CORE: core_w, CHIP: chip_w[:cut], CHIP ^ CORE: relay_w}
    x = filled[:, :capacity].reshape(copies * n, 2 * width)
    x_near = swap(x[:n], CHIP)

    core_out = pre((w[1], w[3]), BF16)
    core_in = swap(jnp.concatenate(core_out, axis=0), CORE)
    keep = pre((w[0], w[2]), F32)
    chip_in = swap((keep[1] + core_in[n:].astype(F32)).astype(BF16), CHIP)
    (h0,) = call(
        act_body, [sds((n, 3 * units), BF16)], [keep[0], core_in[:n], chip_in], 0
    )
    h2 = swap(h0, CHIP)
    h1 = swap(h0, CORE)
    (acc,) = call(
        functools.partial(result_body, True),
        [sds((copies * n, 2 * width), F32)],
        [h0, h1, w[0], w[1]],
        2 * copies * per_pair,
        me,
    )
    h2, acc, last = lax.optimization_barrier((h2, acc, x[n:]))
    h3 = swap(h2, CORE)
    x_far = swap(last, CHIP)
    (result,) = call(
        functools.partial(result_body, False),
        [sds((copies * n, 2 * width), BF16)],
        [h2, h3, w[2], w[3], acc],
        2 * copies * per_pair,
        me,
    )
    returned = there_and_back(result.reshape(copies * experts, capacity, 2 * width))
    kept, share = call(
        weight_grads_body,
        [sds((4 * width, 3 * units), BF16)] * 2,
        [x, x_near, x_far, h0, h1],
        8 * per_pair,
        me,
    )
    got = swap(share, CORE)
    gate_grad, up_grad, down_grad = call(
        merge_body,
        [sds((model, units), BF16), sds((model, units), BF16), sds((units, model), BF16)],
        [kept, got],
        0,
        me,
    )
    layer_out, grad_tokens = call(
        combine_body,
        [sds((rows, width), BF16), sds((rows, width), BF16)],
        [pos, gate_probs, returned.reshape(copies * n, 2 * width)],
        8 * copies * n * rows * width,
    )
    return layer_out, grad_tokens, gate_grad[None], up_grad[None], down_grad[None]


def solution(mesh):
    experts = mesh.shape["expert"]
    fine = Mesh(mesh.devices.reshape(2, 2, 2, experts), (*DP, "expert"))
    return jax.shard_map(
        per_device,
        mesh=fine,
        in_specs=(
            P("expert", DP),
            P("expert", DP),
            P("expert", None),
            P("expert", None),
            P("expert", None, DP),
            P("expert", None, DP),
            P("expert", DP, None),
        ),
        out_specs=(
            P("expert", DP),
            P("expert", DP),
            P("expert", None, DP),
            P("expert", None, DP),
            P("expert", DP, None),
        ),
        check_vma=False,
    )
```

```python
import functools

import jax
import jax.numpy as jnp
from jax import lax
from jax.experimental import pallas as pl
from jax.experimental.pallas import tpu as pltpu
from jax.sharding import Mesh
from jax.sharding import PartitionSpec as P


BF16, F32, I32 = jnp.bfloat16, jnp.float32, jnp.int32
PAD = 8
DP = ("za", "zb", "core")
FAR, CHIP, CORE = 4, 2, 1
FEATURES = (0, FAR)


def dot(a, b, ca=1, cb=0):
    return lax.dot_general(a, b, (((ca,), (cb,)), ((), ())), preferred_element_type=F32)


def call(body, outs, args, flops, me=None):
    moved = sum(a.size * a.dtype.itemsize for a in args)
    moved += sum(o.size * o.dtype.itemsize for o in outs)
    vmem, smem = pl.BlockSpec(memory_space=pltpu.VMEM), pl.BlockSpec(memory_space=pltpu.SMEM)
    head = [] if me is None else [me]
    return pl.pallas_call(
        body,
        out_shape=outs,
        in_specs=[smem] * len(head) + [vmem] * len(args),
        out_specs=[vmem] * len(outs),
        cost_estimate=pl.CostEstimate(flops=flops, bytes_accessed=moved, transcendentals=0),
        compiler_params=pltpu.CompilerParams(vmem_limit_bytes=16 << 20),
    )(*head, *args)


def iota(shape, dim):
    return lax.broadcasted_iota(I32, shape, dim)


def route_body(experts, capacity, ids_ref, probs_ref, tok_ref, grad_ref, out_ref, pos_ref):
    ids, probs = ids_ref[...], probs_ref[...]
    rows = ids.shape[1]
    width = tok_ref.shape[1]
    named = [iota((experts, rows), 0) == ids[k : k + 1, :] for k in range(2)]
    both = (named[0].astype(F32) + named[1].astype(F32)).astype(BF16)
    earlier = (iota((rows, rows), 0) < iota((rows, rows), 1)).astype(F32).astype(BF16)
    before = dot(both, earlier)
    place = iota((experts * PAD, rows), 0)
    here = []
    for k in range(2):
        slot = jnp.sum(jnp.where(named[k], before, 0.0), axis=0, keepdims=True).astype(I32)
        pos_ref[k : k + 1, :] = ids[k : k + 1, :] * capacity + slot
        here.append(place == ids[k : k + 1, :] * PAD + slot)
    picks = (here[0] | here[1]).astype(F32).astype(BF16)
    factor = jnp.sum(
        jnp.where(here[0], probs[0:1, :], jnp.where(here[1], probs[1:2, :], 0.0)),
        axis=1,
        keepdims=True,
    )
    routed = dot(picks, tok_ref[...]).astype(BF16)
    routed_grad = (dot(picks, grad_ref[...]) * factor).astype(BF16)
    for i in range(len(FEATURES)):
        at = pl.ds(i * experts * PAD, experts * PAD)
        out_ref[at, :width] = routed
        out_ref[at, width:] = routed_grad


def combine_body(pos_ref, probs_ref, back_ref, out_ref, grad_ref):
    pos, probs = pos_ref[...], probs_ref[...]
    rows = pos.shape[1]
    width = out_ref.shape[1]
    n = back_ref.shape[0] // len(FEATURES)
    place = iota((n, rows), 0)
    sums = []
    for k in range(2):
        pick = (place == pos[k : k + 1, :]).astype(F32).astype(BF16)
        sums.append(
            sum(dot(pick, back_ref[pl.ds(i * n, n), :], 0, 0) for i in range(len(FEATURES)))
        )
    out_ref[...] = (sums[0][:, :width] * probs[:, 0:1] + sums[1][:, :width] * probs[:, 1:2]).astype(
        BF16
    )
    grad_ref[...] = (sums[0][:, width:] + sums[1][:, width:]).astype(BF16)


def block_of(me_ref, mask, width):
    return pl.ds(pl.multiple_of((me_ref[0] ^ mask) * width, width), width)


def half_of(me_ref, i, n):
    far = jnp.where((me_ref[0] & FAR) == 0, i, 1 - i)
    return pl.ds(pl.multiple_of(far * n, n), n)


def pack_body(masks, me_ref, gate_ref, up_ref, down_ref, out_ref):
    width = out_ref.shape[0] // len(masks)
    units = gate_ref.shape[1]
    for i, mask in enumerate(masks):
        at, to = block_of(me_ref, mask, width), pl.ds(i * width, width)
        out_ref[to, :units] = gate_ref[at, :]
        out_ref[to, units : 2 * units] = up_ref[at, :]
        out_ref[to, 2 * units :] = down_ref[:, at].T


def pre_body(me_ref, x_ref, first_ref, second_ref, *out_refs):
    n = x_ref.shape[0] // len(FEATURES)
    width = x_ref.shape[1] // 2
    units = first_ref.shape[1] // 3
    pres, hids = [0.0, 0.0], 0.0
    for i in range(len(FEATURES)):
        rows, w = half_of(me_ref, i, n), pl.ds(i * width, width)
        x, g = x_ref[rows, :width], x_ref[rows, width:]
        for j, ref in enumerate((first_ref, second_ref)):
            pres[j] = pres[j] + dot(x, ref[w, : 2 * units])
        downs = jnp.concatenate([first_ref[w, 2 * units :], second_ref[w, 2 * units :]], axis=1)
        hids = hids + dot(g, downs)
    for j in range(2):
        ref, at = (out_refs[0], pl.ds(j * n, n)) if len(out_refs) == 1 else (out_refs[j], pl.ds(0, n))
        ref[at, : 2 * units] = pres[j].astype(ref.dtype)
        ref[at, 2 * units :] = hids[:, j * units : (j + 1) * units].astype(ref.dtype)


def act_body(keep_ref, core_ref, chip_ref, out_ref):
    units = keep_ref.shape[1] // 3
    n = keep_ref.shape[0]
    pre = keep_ref[...] + core_ref[pl.ds(0, n), :].astype(F32) + chip_ref[...].astype(F32)
    gate, up, hid = pre[:, :units], pre[:, units : 2 * units], pre[:, 2 * units :]
    sig = jax.nn.sigmoid(gate)
    silu = gate * sig
    out_ref[:, :units] = (silu * up).astype(BF16)
    out_ref[:, units : 2 * units] = (hid * up * sig * (1.0 + gate * (1.0 - sig))).astype(BF16)
    out_ref[:, 2 * units :] = (hid * silu).astype(BF16)


def result_body(first, me_ref, *refs):
    h_refs, w_refs = refs[:2], refs[2:4]
    acc_ref, out_ref = (None, refs[4]) if first else (refs[4], refs[5])
    n = h_refs[0].shape[0]
    units = h_refs[0].shape[1] // 3
    width = out_ref.shape[1] // 2
    hidden = jnp.concatenate([h[:, :units] for h in h_refs], axis=1)
    grads = jnp.concatenate([h[:, units:] for h in h_refs], axis=1)
    for i in range(len(FEATURES)):
        w = pl.ds(i * width, width)
        downs = jnp.concatenate([r[w, 2 * units :] for r in w_refs], axis=1)
        pairs = jnp.concatenate([r[w, : 2 * units] for r in w_refs], axis=1)
        out, back = dot(hidden, downs, 1, 1), dot(grads, pairs, 1, 1)
        if first:
            rows = pl.ds(i * n, n)
            out_ref[rows, :width] = out
            out_ref[rows, width:] = back
        else:
            rows, held = half_of(me_ref, i, n), pl.ds(i * n, n)
            out_ref[rows, :width] = (out + acc_ref[held, :width]).astype(BF16)
            out_ref[rows, width:] = (back + acc_ref[held, width:]).astype(BF16)


def weight_grads_body(me_ref, own_ref, near_ref, far_ref, h0_ref, h1_ref, keep_ref, send_ref):
    n = near_ref.shape[0]
    width = own_ref.shape[1] // 2
    units = h0_ref.shape[1] // 3
    grads = jnp.concatenate([h0_ref[:, units:], h1_ref[:, units:]], axis=1)
    hidden = jnp.concatenate([h0_ref[:, :units], h1_ref[:, :units]], axis=1)

    def work(x, g, to):
        both, down = dot(x, grads, 0, 0).astype(BF16), dot(g, hidden, 0, 0).astype(BF16)
        keep_ref[to, : 2 * units], send_ref[to, : 2 * units] = both[:, : 2 * units], both[:, 2 * units :]
        keep_ref[to, 2 * units :], send_ref[to, 2 * units :] = down[:, :units], down[:, units:]

    for i in range(len(FEATURES)):
        rows = pl.ds(i * n, n)
        work(own_ref[rows, :width], own_ref[rows, width:], pl.ds(i * width, width))
    for i, ref in enumerate((near_ref, far_ref)):
        at = pl.ds((len(FEATURES) + i) * width, width)
        work(ref[:, :width], ref[:, width:], at)


def merge_body(me_ref, keep_ref, got_ref, gate_ref, up_ref, down_ref):
    units = gate_ref.shape[1]
    width = keep_ref.shape[0] // 4
    for core, ref in ((0, keep_ref), (CORE, got_ref)):
        for i in range(4):
            block = ((me_ref[0] ^ core ^ (CHIP if i >= 2 else 0)) & (FAR - 1)) + FAR * (i % 2)
            at = pl.ds(pl.multiple_of(block * width, width), width)
            w = pl.ds(i * width, width)
            gate_ref[at, :] = ref[w, :units]
            up_ref[at, :] = ref[w, units : 2 * units]
            down_ref[:, at] = ref[w, 2 * units :].T


def per_device(tokens, grad_out, expert_ids, gate_probs, gate_weight, up_weight, down_weight):
    experts = lax.axis_size("expert")
    rows, width = tokens.shape
    capacity = max(2, 3 * rows // experts)
    n, copies = experts * capacity, len(FEATURES)
    gate, up, down = gate_weight[0], up_weight[0], down_weight[0]
    units, model = down.shape
    me = lax.axis_index(DP).astype(I32).reshape(1)
    sds = jax.ShapeDtypeStruct
    per_pair = 6 * n * width * units

    def swap(x, mask):
        return lax.ppermute(x, DP, [(j, j ^ mask) for j in range(8)])

    def pack(*masks):
        return call(
            functools.partial(pack_body, masks),
            [sds((len(masks) * width, 3 * units), BF16)],
            [gate, up, down],
            0,
            me,
        )[0]

    def pre(weights, outs):
        return call(pre_body, outs, [x, *weights], 2 * copies * per_pair, me)

    def there_and_back(a):
        return lax.all_to_all(a, ("za", "expert"), split_axis=0, concat_axis=0, tiled=True)

    cut = copies * width
    chip_w = swap(pack(CHIP, CHIP ^ FAR, CHIP ^ CORE, CHIP ^ CORE ^ FAR), CHIP)
    send, pos = call(
        functools.partial(route_body, experts, capacity),
        [sds((copies * experts * PAD, 2 * width), BF16), sds((2, rows), I32)],
        [expert_ids.T, gate_probs.T, tokens, grad_out],
        4 * experts * PAD * rows * width,
    )
    filled = there_and_back(send.reshape(copies * experts, PAD, 2 * width))
    near = pack(0, FAR, CORE, CORE ^ FAR)
    core_w = swap(near[cut:], CORE)
    relay_w = swap(chip_w[cut:], CORE)
    filled, near, core_w, chip_w, relay_w = lax.optimization_barrier(
        (filled, near, core_w, chip_w, relay_w)
    )
    w = {0: near, CORE: core_w, CHIP: chip_w, CHIP ^ CORE: relay_w}
    x = filled[:, :capacity].reshape(copies * n, 2 * width)
    x_near = swap(x[:n], CHIP)

    (core_out,) = pre((w[1], w[3]), [sds((2 * n, 3 * units), BF16)])
    core_in = swap(core_out, CORE)
    keep = pre((w[0], w[2]), [sds((n, 3 * units), F32)] * 2)
    chip_in = swap((keep[1] + core_in[n:].astype(F32)).astype(BF16), CHIP)
    (h0,) = call(act_body, [sds((n, 3 * units), BF16)], [keep[0], core_in, chip_in], 0)
    h2 = swap(h0, CHIP)
    h1 = swap(h0, CORE)
    (acc,) = call(
        functools.partial(result_body, True),
        [sds((copies * n, 2 * width), F32)],
        [h0, h1, w[0], w[1]],
        2 * copies * per_pair,
        me,
    )
    h2, acc, last = lax.optimization_barrier((h2, acc, x[n:]))
    h3 = swap(h2, CORE)
    x_far = swap(last, CHIP)
    (result,) = call(
        functools.partial(result_body, False),
        [sds((copies * n, 2 * width), BF16)],
        [h2, h3, w[2], w[3], acc],
        2 * copies * per_pair,
        me,
    )
    returned = there_and_back(result.reshape(copies * experts, capacity, 2 * width))
    kept, share = call(
        weight_grads_body,
        [sds((4 * width, 3 * units), BF16)] * 2,
        [x, x_near, x_far, h0, h1],
        8 * per_pair,
        me,
    )
    got = swap(share, CORE)
    gate_grad, up_grad, down_grad = call(
        merge_body,
        [sds((model, units), BF16), sds((model, units), BF16), sds((units, model), BF16)],
        [kept, got],
        0,
        me,
    )
    layer_out, grad_tokens = call(
        combine_body,
        [sds((rows, width), BF16), sds((rows, width), BF16)],
        [pos, gate_probs, returned.reshape(copies * n, 2 * width)],
        8 * copies * n * rows * width,
    )
    return layer_out, grad_tokens, gate_grad[None], up_grad[None], down_grad[None]


def solution(mesh):
    experts = mesh.shape["expert"]
    fine = Mesh(mesh.devices.reshape(2, 2, 2, experts), (*DP, "expert"))
    return jax.shard_map(
        per_device,
        mesh=fine,
        in_specs=(
            P("expert", DP),
            P("expert", DP),
            P("expert", None),
            P("expert", None),
            P("expert", None, DP),
            P("expert", None, DP),
            P("expert", DP, None),
        ),
        out_specs=(
            P("expert", DP),
            P("expert", DP),
            P("expert", None, DP),
            P("expert", None, DP),
            P("expert", DP, None),
        ),
        check_vma=False,
    )
```

```python
import functools

import jax
import jax.numpy as jnp
from jax import lax
from jax.experimental import pallas as pl
from jax.experimental.pallas import tpu as pltpu
from jax.sharding import Mesh
from jax.sharding import PartitionSpec as P


BF16, F32, I32 = jnp.bfloat16, jnp.float32, jnp.int32
DP = ("za", "zb", "core")
SMALL = pltpu.CompilerParams(vmem_limit_bytes=16 << 20)
FAR, CHIP, CORE = 4, 2, 1
FEATURES = (0, FAR)


def dot(a, b, ca=1, cb=0):
    return lax.dot_general(a, b, (((ca,), (cb,)), ((), ())), preferred_element_type=F32)


def call(body, outs, args, flops, me=None):
    moved = sum(a.size * a.dtype.itemsize for a in args)
    moved += sum(o.size * o.dtype.itemsize for o in outs)
    vmem, smem = pl.BlockSpec(memory_space=pltpu.VMEM), pl.BlockSpec(memory_space=pltpu.SMEM)
    head = [] if me is None else [me]
    return pl.pallas_call(
        body,
        out_shape=outs,
        in_specs=[smem] * len(head) + [vmem] * len(args),
        out_specs=[vmem] * len(outs),
        cost_estimate=pl.CostEstimate(flops=flops, bytes_accessed=moved, transcendentals=0),
        compiler_params=SMALL,
    )(*head, *args)


def iota(shape, dim):
    return lax.broadcasted_iota(I32, shape, dim)


def route_body(experts, piece, ids_ref, probs_ref, tok_ref, grad_ref, out_ref, pos_ref):
    ids, probs = ids_ref[...], probs_ref[...]
    rows = ids.shape[1]
    width = tok_ref.shape[1]
    named = [iota((experts, rows), 0) == ids[k : k + 1, :] for k in range(2)]
    both = (named[0].astype(F32) + named[1].astype(F32)).astype(BF16)
    earlier = (iota((rows, rows), 0) < iota((rows, rows), 1)).astype(F32).astype(BF16)
    before = dot(both, earlier)
    place = iota((experts * piece, rows), 0)
    here = []
    for k in range(2):
        slot = jnp.sum(jnp.where(named[k], before, 0.0), axis=0, keepdims=True).astype(I32)
        pos = ids[k : k + 1, :] * piece + slot
        pos_ref[k : k + 1, :] = pos
        here.append(place == pos)
    picks = (here[0] | here[1]).astype(F32).astype(BF16)
    factor = jnp.sum(
        jnp.where(here[0], probs[0:1, :], jnp.where(here[1], probs[1:2, :], 0.0)),
        axis=1,
        keepdims=True,
    )
    routed = dot(picks, tok_ref[...]).astype(BF16)
    routed_grad = (dot(picks, grad_ref[...]) * factor).astype(BF16)
    for i in range(len(FEATURES)):
        at = pl.ds(i * experts * piece, experts * piece)
        out_ref[at, :width] = routed
        out_ref[at, width:] = routed_grad


def combine_body(pos_ref, probs_ref, back_ref, out_ref, grad_ref):
    pos, probs = pos_ref[...], probs_ref[...]
    rows = pos.shape[1]
    width = out_ref.shape[1]
    n = back_ref.shape[0] // len(FEATURES)
    place = iota((n, rows), 0)
    sums = []
    for k in range(2):
        pick = (place == pos[k : k + 1, :]).astype(F32).astype(BF16)
        sums.append(
            sum(dot(pick, back_ref[pl.ds(i * n, n), :], 0, 0) for i in range(len(FEATURES)))
        )
    out_ref[...] = (sums[0][:, :width] * probs[:, 0:1] + sums[1][:, :width] * probs[:, 1:2]).astype(
        BF16
    )
    grad_ref[...] = (sums[0][:, width:] + sums[1][:, width:]).astype(BF16)


def block_of(me_ref, mask, width):
    return pl.ds(pl.multiple_of((me_ref[0] ^ mask) * width, width), width)


def half_of(me_ref, i, n):
    far = jnp.where((me_ref[0] & FAR) == 0, i, 1 - i)
    return pl.ds(pl.multiple_of(far * n, n), n)


def pack_body(masks, me_ref, gate_ref, up_ref, down_ref, out_ref, downs, sems):
    width = out_ref.shape[0] // len(masks)
    units = gate_ref.shape[1]
    fetches = []
    for i, mask in enumerate(masks):
        at, to = block_of(me_ref, mask, width), pl.ds(i * width, width)
        pairs = (
            (down_ref.at[:, at], downs.at[i]),
            (gate_ref.at[at, :], out_ref.at[to, :units]),
            (up_ref.at[at, :], out_ref.at[to, units : 2 * units]),
        )
        for k, (source, target) in enumerate(pairs):
            fetches.append(pltpu.make_async_copy(source, target, sems.at[3 * i + k]))
            fetches[-1].start()
    for i in range(len(masks)):
        fetches[3 * i].wait()
        out_ref[pl.ds(i * width, width), 2 * units :] = downs[i].T
    for i in range(len(masks)):
        fetches[3 * i + 1].wait()
        fetches[3 * i + 2].wait()


def pre_body(me_ref, x_ref, first_ref, second_ref, *out_refs):
    n = x_ref.shape[0] // len(FEATURES)
    width = x_ref.shape[1] // 2
    units = first_ref.shape[1] // 3
    pres, hids = [0.0, 0.0], 0.0
    for i in range(len(FEATURES)):
        rows, w = half_of(me_ref, i, n), pl.ds(i * width, width)
        x, g = x_ref[rows, :width], x_ref[rows, width:]
        for j, ref in enumerate((first_ref, second_ref)):
            pres[j] = pres[j] + dot(x, ref[w, : 2 * units])
        downs = jnp.concatenate([first_ref[w, 2 * units :], second_ref[w, 2 * units :]], axis=1)
        hids = hids + dot(g, downs)
    for j in range(2):
        ref, at = (out_refs[0], pl.ds(j * n, n)) if len(out_refs) == 1 else (out_refs[j], pl.ds(0, n))
        ref[at, : 2 * units] = pres[j].astype(ref.dtype)
        ref[at, 2 * units :] = hids[:, j * units : (j + 1) * units].astype(ref.dtype)


def act_body(keep_ref, core_ref, chip_ref, out_ref):
    units = keep_ref.shape[1] // 3
    n = keep_ref.shape[0]
    pre = keep_ref[...] + core_ref[pl.ds(0, n), :].astype(F32) + chip_ref[...].astype(F32)
    gate, up, hid = pre[:, :units], pre[:, units : 2 * units], pre[:, 2 * units :]
    sig = jax.nn.sigmoid(gate)
    silu = gate * sig
    out_ref[:, :units] = (silu * up).astype(BF16)
    out_ref[:, units : 2 * units] = (hid * up * sig * (1.0 + gate * (1.0 - sig))).astype(BF16)
    out_ref[:, 2 * units :] = (hid * silu).astype(BF16)


def result_body(first, me_ref, *refs):
    h_refs, w_refs = refs[:2], refs[2:4]
    acc_ref, out_ref = (None, refs[4]) if first else (refs[4], refs[5])
    n = h_refs[0].shape[0]
    units = h_refs[0].shape[1] // 3
    width = out_ref.shape[1] // 2
    hidden = jnp.concatenate([h[:, :units] for h in h_refs], axis=1)
    grads = jnp.concatenate([h[:, units:] for h in h_refs], axis=1)
    for i in range(len(FEATURES)):
        w = pl.ds(i * width, width)
        downs = jnp.concatenate([r[w, 2 * units :] for r in w_refs], axis=1)
        pairs = jnp.concatenate([r[w, : 2 * units] for r in w_refs], axis=1)
        out, back = dot(hidden, downs, 1, 1), dot(grads, pairs, 1, 1)
        if first:
            rows = pl.ds(i * n, n)
            out_ref[rows, :width] = out
            out_ref[rows, width:] = back
        else:
            rows, held = half_of(me_ref, i, n), pl.ds(i * n, n)
            out_ref[rows, :width] = (out + acc_ref[held, :width]).astype(BF16)
            out_ref[rows, width:] = (back + acc_ref[held, width:]).astype(BF16)


def weight_grads_body(own_ref, first_ref, last_ref, h0_ref, h1_ref, keep_ref, send_ref):
    n = h0_ref.shape[0]
    parts = [(own_ref, pl.ds(i * n, n)) for i in range(len(FEATURES))]
    parts += [(first_ref, pl.ds(0, n)), (last_ref, pl.ds(0, n))]
    width = own_ref.shape[1] // 2
    units = h0_ref.shape[1] // 3
    grads = jnp.concatenate([h0_ref[:, units:], h1_ref[:, units:]], axis=1)
    hidden = jnp.concatenate([h0_ref[:, :units], h1_ref[:, :units]], axis=1)
    for i, (ref, rows) in enumerate(parts):
        to = pl.ds(i * width, width)
        both = dot(ref[rows, :width], grads, 0, 0).astype(BF16)
        down = dot(ref[rows, width:], hidden, 0, 0).astype(BF16)
        keep_ref[to, : 2 * units], send_ref[to, : 2 * units] = both[:, : 2 * units], both[:, 2 * units :]
        keep_ref[to, 2 * units :], send_ref[to, 2 * units :] = down[:, :units], down[:, units:]


def merge_body(me_ref, keep_ref, got_ref, gate_ref, up_ref, down_ref):
    units = gate_ref.shape[1]
    width = keep_ref.shape[0] // 4
    for core, ref in ((0, keep_ref), (CORE, got_ref)):
        for i in range(4):
            block = ((me_ref[0] ^ core ^ (CHIP if i >= 2 else 0)) & (FAR - 1)) + FAR * (i % 2)
            at = pl.ds(pl.multiple_of(block * width, width), width)
            w = pl.ds(i * width, width)
            gate_ref[at, :] = ref[w, :units]
            up_ref[at, :] = ref[w, units : 2 * units]
            down_ref[:, at] = ref[w, 2 * units :].T


def per_device(tokens, grad_out, expert_ids, gate_probs, gate_weight, up_weight, down_weight):
    experts = lax.axis_size("expert")
    rows, width = tokens.shape
    capacity = max(2, 3 * rows // experts)
    piece = -(-capacity // 8) * 8
    n, copies = experts * piece, len(FEATURES)
    gate, up, down = gate_weight[0], up_weight[0], down_weight[0]
    units, model = down.shape
    me = lax.axis_index(DP).astype(I32).reshape(1)
    sds = jax.ShapeDtypeStruct
    per_pair = 6 * n * width * units

    def swap(x, mask):
        return lax.ppermute(x, DP, [(j, j ^ mask) for j in range(8)])

    def pack(*masks, params=None):
        space = pl.BlockSpec(memory_space=pl.ANY)
        return pl.pallas_call(
            functools.partial(pack_body, masks),
            out_shape=sds((len(masks) * width, 3 * units), BF16),
            in_specs=[pl.BlockSpec(memory_space=pltpu.SMEM), space, space, space],
            out_specs=pl.BlockSpec(memory_space=pltpu.VMEM),
            scratch_shapes=[
                pltpu.VMEM((len(masks), units, width), BF16),
                pltpu.SemaphoreType.DMA((3 * len(masks),)),
            ],
            cost_estimate=pl.CostEstimate(
                flops=0, bytes_accessed=12 * len(masks) * width * units, transcendentals=0
            ),
            compiler_params=params,
        )(me, gate, up, down)

    def pre(weights, outs):
        return call(pre_body, outs, [x, *weights], 2 * copies * per_pair, me)

    def there_and_back(a):
        return lax.all_to_all(a, ("za", "expert"), split_axis=0, concat_axis=0, tiled=True)

    cut = copies * width
    chip_w = swap(pack(CHIP, CHIP ^ FAR, CHIP ^ CORE, CHIP ^ CORE ^ FAR), CHIP)
    send, pos = call(
        functools.partial(route_body, experts, piece),
        [sds((copies * n, 2 * width), BF16), sds((2, rows), I32)],
        [expert_ids.T, gate_probs.T, tokens, grad_out],
        4 * n * rows * width,
    )
    filled = there_and_back(send.reshape(copies * experts, piece, 2 * width))
    near = pack(0, FAR, CORE, CORE ^ FAR, params=SMALL)
    core_w = swap(near[cut:], CORE)
    relay_w = swap(chip_w[cut:], CORE)
    filled, near, core_w, chip_w, relay_w = lax.optimization_barrier(
        (filled, near, core_w, chip_w, relay_w)
    )
    w = {0: near, CORE: core_w, CHIP: chip_w, CHIP ^ CORE: relay_w}
    x = filled.reshape(copies * n, 2 * width)
    x_first = swap(x[:n], CHIP)

    (core_out,) = pre((w[1], w[3]), [sds((2 * n, 3 * units), BF16)])
    core_in = swap(core_out, CORE)
    keep = pre((w[0], w[2]), [sds((n, 3 * units), F32)] * 2)
    chip_in = swap((keep[1] + core_in[n:].astype(F32)).astype(BF16), CHIP)
    (h0,) = call(act_body, [sds((n, 3 * units), BF16)], [keep[0], core_in, chip_in], 0)
    h2 = swap(h0, CHIP)
    h1 = swap(h0, CORE)
    (acc,) = call(
        functools.partial(result_body, True),
        [sds((copies * n, 2 * width), F32)],
        [h0, h1, w[0], w[1]],
        2 * copies * per_pair,
        me,
    )
    h2, acc, last = lax.optimization_barrier((h2, acc, x[n:]))
    h3 = swap(h2, CORE)
    x_last = swap(last, CHIP)
    (result,) = call(
        functools.partial(result_body, False),
        [sds((copies * n, 2 * width), BF16)],
        [h2, h3, w[2], w[3], acc],
        2 * copies * per_pair,
        me,
    )
    returned = there_and_back(result.reshape(copies * experts, piece, 2 * width))
    kept, share = call(
        weight_grads_body,
        [sds((4 * width, 3 * units), BF16)] * 2,
        [x, x_first, x_last, h0, h1],
        8 * per_pair,
    )
    got = swap(share, CORE)
    gate_grad, up_grad, down_grad = call(
        merge_body,
        [sds((model, units), BF16), sds((model, units), BF16), sds((units, model), BF16)],
        [kept, got],
        0,
        me,
    )
    layer_out, grad_tokens = call(
        combine_body,
        [sds((rows, width), BF16), sds((rows, width), BF16)],
        [pos, gate_probs, returned.reshape(copies * n, 2 * width)],
        8 * copies * n * rows * width,
    )
    return layer_out, grad_tokens, gate_grad[None], up_grad[None], down_grad[None]


def solution(mesh):
    experts = mesh.shape["expert"]
    fine = Mesh(mesh.devices.reshape(2, 2, 2, experts), (*DP, "expert"))
    return jax.shard_map(
        per_device,
        mesh=fine,
        in_specs=(
            P("expert", DP),
            P("expert", DP),
            P("expert", None),
            P("expert", None),
            P("expert", None, DP),
            P("expert", None, DP),
            P("expert", DP, None),
        ),
        out_specs=(
            P("expert", DP),
            P("expert", DP),
            P("expert", None, DP),
            P("expert", None, DP),
            P("expert", DP, None),
        ),
        check_vma=False,
    )
```

```python
import functools

import jax
import jax.numpy as jnp
from jax import lax
from jax.experimental import pallas as pl
from jax.experimental.pallas import tpu as pltpu
from jax.sharding import Mesh
from jax.sharding import PartitionSpec as P


BF16, F32, I32 = jnp.bfloat16, jnp.float32, jnp.int32
DP = ("za", "zb", "core")
SMALL = pltpu.CompilerParams(vmem_limit_bytes=16 << 20)
FAR, CHIP, CORE = 4, 2, 1
FEATURES = (0, FAR)


def dot(a, b, ca=1, cb=0):
    return lax.dot_general(a, b, (((ca,), (cb,)), ((), ())), preferred_element_type=F32)


def call(body, outs, args, flops, me=None):
    moved = sum(a.size * a.dtype.itemsize for a in args)
    moved += sum(o.size * o.dtype.itemsize for o in outs)
    vmem, smem = pl.BlockSpec(memory_space=pltpu.VMEM), pl.BlockSpec(memory_space=pltpu.SMEM)
    head = [] if me is None else [me]
    return pl.pallas_call(
        body,
        out_shape=outs,
        in_specs=[smem] * len(head) + [vmem] * len(args),
        out_specs=[vmem] * len(outs),
        cost_estimate=pl.CostEstimate(flops=flops, bytes_accessed=moved, transcendentals=0),
        compiler_params=SMALL,
    )(*head, *args)


def iota(shape, dim):
    return lax.broadcasted_iota(I32, shape, dim)


def route_body(experts, piece, ids_ref, probs_ref, tok_ref, grad_ref, out_ref, pos_ref):
    ids, probs = ids_ref[...], probs_ref[...]
    rows = ids.shape[1]
    width = tok_ref.shape[1]
    named = [iota((experts, rows), 0) == ids[k : k + 1, :] for k in range(2)]
    both = (named[0].astype(F32) + named[1].astype(F32)).astype(BF16)
    earlier = (iota((rows, rows), 0) < iota((rows, rows), 1)).astype(F32).astype(BF16)
    before = dot(both, earlier)
    place = iota((experts * piece, rows), 0)
    here = []
    for k in range(2):
        slot = jnp.sum(jnp.where(named[k], before, 0.0), axis=0, keepdims=True).astype(I32)
        pos = ids[k : k + 1, :] * piece + slot
        pos_ref[k : k + 1, :] = pos
        here.append(place == pos)
    picks = (here[0] | here[1]).astype(F32).astype(BF16)
    factor = jnp.sum(
        jnp.where(here[0], probs[0:1, :], jnp.where(here[1], probs[1:2, :], 0.0)),
        axis=1,
        keepdims=True,
    )
    routed = dot(picks, tok_ref[...]).astype(BF16)
    routed_grad = (dot(picks, grad_ref[...]) * factor).astype(BF16)
    for i in range(len(FEATURES)):
        at = pl.ds(i * experts * piece, experts * piece)
        out_ref[at, :width] = routed
        out_ref[at, width:] = routed_grad


def combine_body(pos_ref, probs_ref, back_ref, out_ref, grad_ref):
    pos, probs = pos_ref[...], probs_ref[...]
    rows = pos.shape[1]
    width = out_ref.shape[1]
    n = back_ref.shape[0] // len(FEATURES)
    place = iota((n, rows), 0)
    sums = []
    for k in range(2):
        pick = (place == pos[k : k + 1, :]).astype(F32).astype(BF16)
        sums.append(
            sum(dot(pick, back_ref[pl.ds(i * n, n), :], 0, 0) for i in range(len(FEATURES)))
        )
    out_ref[...] = (sums[0][:, :width] * probs[:, 0:1] + sums[1][:, :width] * probs[:, 1:2]).astype(
        BF16
    )
    grad_ref[...] = (sums[0][:, width:] + sums[1][:, width:]).astype(BF16)


def block_of(me_ref, mask, width):
    return pl.ds(pl.multiple_of((me_ref[0] ^ mask) * width, width), width)


def half_of(me_ref, i, n):
    far = jnp.where((me_ref[0] & FAR) == 0, i, 1 - i)
    return pl.ds(pl.multiple_of(far * n, n), n)


def pack_body(masks, me_ref, gate_ref, up_ref, down_ref, out_ref, downs, sems):
    width = out_ref.shape[0] // len(masks)
    units = gate_ref.shape[1]
    fetches = []
    for i, mask in enumerate(masks):
        at, to = block_of(me_ref, mask, width), pl.ds(i * width, width)
        pairs = (
            (down_ref.at[:, at], downs.at[i]),
            (gate_ref.at[at, :], out_ref.at[to, :units]),
            (up_ref.at[at, :], out_ref.at[to, units : 2 * units]),
        )
        for k, (source, target) in enumerate(pairs):
            fetches.append(pltpu.make_async_copy(source, target, sems.at[3 * i + k]))
            fetches[-1].start()
    for i in range(len(masks)):
        fetches[3 * i].wait()
        out_ref[pl.ds(i * width, width), 2 * units :] = downs[i].T
    for i in range(len(masks)):
        fetches[3 * i + 1].wait()
        fetches[3 * i + 2].wait()


def pre_body(me_ref, x_ref, first_ref, second_ref, *out_refs):
    n = x_ref.shape[0] // len(FEATURES)
    width = x_ref.shape[1] // 2
    units = first_ref.shape[1] // 3
    pres, hids = [0.0, 0.0], 0.0
    for i in range(len(FEATURES)):
        rows, w = half_of(me_ref, i, n), pl.ds(i * width, width)
        x, g = x_ref[rows, :width], x_ref[rows, width:]
        for j, ref in enumerate((first_ref, second_ref)):
            pres[j] = pres[j] + dot(x, ref[w, : 2 * units])
        downs = jnp.concatenate([first_ref[w, 2 * units :], second_ref[w, 2 * units :]], axis=1)
        hids = hids + dot(g, downs)
    for j in range(2):
        ref, at = (out_refs[0], pl.ds(j * n, n)) if len(out_refs) == 1 else (out_refs[j], pl.ds(0, n))
        ref[at, : 2 * units] = pres[j].astype(ref.dtype)
        ref[at, 2 * units :] = hids[:, j * units : (j + 1) * units].astype(ref.dtype)


def act_body(keep_ref, core_ref, chip_ref, out_ref):
    units = keep_ref.shape[1] // 3
    n = keep_ref.shape[0]
    pre = keep_ref[...] + core_ref[pl.ds(0, n), :].astype(F32) + chip_ref[...].astype(F32)
    gate, up, hid = pre[:, :units], pre[:, units : 2 * units], pre[:, 2 * units :]
    sig = jax.nn.sigmoid(gate)
    silu = gate * sig
    out_ref[:, :units] = (silu * up).astype(BF16)
    out_ref[:, units : 2 * units] = (hid * up * sig * (1.0 + gate * (1.0 - sig))).astype(BF16)
    out_ref[:, 2 * units :] = (hid * silu).astype(BF16)


def result_body(first, me_ref, *refs):
    h_refs, w_refs = refs[:2], refs[2:4]
    acc_ref, out_ref = (None, refs[4]) if first else (refs[4], refs[5])
    n = h_refs[0].shape[0]
    units = h_refs[0].shape[1] // 3
    width = out_ref.shape[1] // 2
    hidden = jnp.concatenate([h[:, :units] for h in h_refs], axis=1)
    grads = jnp.concatenate([h[:, units:] for h in h_refs], axis=1)
    for i in range(len(FEATURES)):
        w = pl.ds(i * width, width)
        downs = jnp.concatenate([r[w, 2 * units :] for r in w_refs], axis=1)
        pairs = jnp.concatenate([r[w, : 2 * units] for r in w_refs], axis=1)
        out, back = dot(hidden, downs, 1, 1), dot(grads, pairs, 1, 1)
        if first:
            rows = pl.ds(i * n, n)
            out_ref[rows, :width] = out
            out_ref[rows, width:] = back
        else:
            rows, held = half_of(me_ref, i, n), pl.ds(i * n, n)
            out_ref[rows, :width] = (out + acc_ref[held, :width]).astype(BF16)
            out_ref[rows, width:] = (back + acc_ref[held, width:]).astype(BF16)


def weight_grads_body(own_ref, near_ref, h0_ref, h1_ref, keep_ref, send_ref):
    n = h0_ref.shape[0]
    parts = [(ref, pl.ds(i * n, n)) for ref in (own_ref, near_ref) for i in range(len(FEATURES))]
    width = own_ref.shape[1] // 2
    units = h0_ref.shape[1] // 3
    grads = jnp.concatenate([h0_ref[:, units:], h1_ref[:, units:]], axis=1)
    hidden = jnp.concatenate([h0_ref[:, :units], h1_ref[:, :units]], axis=1)
    for i, (ref, rows) in enumerate(parts):
        to = pl.ds(i * width, width)
        both = dot(ref[rows, :width], grads, 0, 0).astype(BF16)
        down = dot(ref[rows, width:], hidden, 0, 0).astype(BF16)
        keep_ref[to, : 2 * units], send_ref[to, : 2 * units] = both[:, : 2 * units], both[:, 2 * units :]
        keep_ref[to, 2 * units :], send_ref[to, 2 * units :] = down[:, :units], down[:, units:]


def merge_body(me_ref, keep_ref, got_ref, gate_ref, up_ref, down_ref):
    units = gate_ref.shape[1]
    width = keep_ref.shape[0] // 4
    for core, ref in ((0, keep_ref), (CORE, got_ref)):
        for i in range(4):
            block = ((me_ref[0] ^ core ^ (CHIP if i >= 2 else 0)) & (FAR - 1)) + FAR * (i % 2)
            at = pl.ds(pl.multiple_of(block * width, width), width)
            w = pl.ds(i * width, width)
            gate_ref[at, :] = ref[w, :units]
            up_ref[at, :] = ref[w, units : 2 * units]
            down_ref[:, at] = ref[w, 2 * units :].T


def per_device(tokens, grad_out, expert_ids, gate_probs, gate_weight, up_weight, down_weight):
    experts = lax.axis_size("expert")
    rows, width = tokens.shape
    capacity = max(2, 3 * rows // experts)
    piece = -(-capacity // 8) * 8
    n, copies = experts * piece, len(FEATURES)
    gate, up, down = gate_weight[0], up_weight[0], down_weight[0]
    units, model = down.shape
    me = lax.axis_index(DP).astype(I32).reshape(1)
    sds = jax.ShapeDtypeStruct
    per_pair = 6 * n * width * units

    def swap(x, mask):
        return lax.ppermute(x, DP, [(j, j ^ mask) for j in range(8)])

    def pack(*masks, params=None):
        space = pl.BlockSpec(memory_space=pl.ANY)
        return pl.pallas_call(
            functools.partial(pack_body, masks),
            out_shape=sds((len(masks) * width, 3 * units), BF16),
            in_specs=[pl.BlockSpec(memory_space=pltpu.SMEM), space, space, space],
            out_specs=pl.BlockSpec(memory_space=pltpu.VMEM),
            scratch_shapes=[
                pltpu.VMEM((len(masks), units, width), BF16),
                pltpu.SemaphoreType.DMA((3 * len(masks),)),
            ],
            cost_estimate=pl.CostEstimate(
                flops=0, bytes_accessed=12 * len(masks) * width * units, transcendentals=0
            ),
            compiler_params=params,
        )(me, gate, up, down)

    def pre(weights, outs):
        return call(pre_body, outs, [x, *weights], 2 * copies * per_pair, me)

    def there_and_back(a):
        return lax.all_to_all(a, ("za", "expert"), split_axis=0, concat_axis=0, tiled=True)

    cut = copies * width
    chip_w = swap(pack(CHIP, CHIP ^ FAR, CHIP ^ CORE, CHIP ^ CORE ^ FAR), CHIP)
    send, pos = call(
        functools.partial(route_body, experts, piece),
        [sds((copies * n, 2 * width), BF16), sds((2, rows), I32)],
        [expert_ids.T, gate_probs.T, tokens, grad_out],
        4 * n * rows * width,
    )
    filled = there_and_back(send.reshape(copies * experts, piece, 2 * width))
    near = pack(0, FAR, CORE, CORE ^ FAR, params=SMALL)
    core_w = swap(near[cut:], CORE)
    relay_w = swap(chip_w[cut:], CORE)
    filled, near, core_w, chip_w, relay_w = lax.optimization_barrier(
        (filled, near, core_w, chip_w, relay_w)
    )
    w = {0: near, CORE: core_w, CHIP: chip_w, CHIP ^ CORE: relay_w}
    x = filled.reshape(copies * n, 2 * width)

    (core_out,) = pre((w[1], w[3]), [sds((2 * n, 3 * units), BF16)])
    core_in = swap(core_out, CORE)
    keep = pre((w[0], w[2]), [sds((n, 3 * units), F32)] * 2)
    chip_in = swap((keep[1] + core_in[n:].astype(F32)).astype(BF16), CHIP)
    (h0,) = call(act_body, [sds((n, 3 * units), BF16)], [keep[0], core_in, chip_in], 0)
    h2 = swap(h0, CHIP)
    h1 = swap(h0, CORE)
    (acc,) = call(
        functools.partial(result_body, True),
        [sds((copies * n, 2 * width), F32)],
        [h0, h1, w[0], w[1]],
        2 * copies * per_pair,
        me,
    )
    x_near = swap(x, CHIP)
    h2, acc = lax.optimization_barrier((h2, acc))
    h3 = swap(h2, CORE)
    (result,) = call(
        functools.partial(result_body, False),
        [sds((copies * n, 2 * width), BF16)],
        [h2, h3, w[2], w[3], acc],
        2 * copies * per_pair,
        me,
    )
    returned = there_and_back(result.reshape(copies * experts, piece, 2 * width))
    kept, share = call(
        weight_grads_body,
        [sds((4 * width, 3 * units), BF16)] * 2,
        [x, x_near, h0, h1],
        8 * per_pair,
    )
    got = swap(share, CORE)
    gate_grad, up_grad, down_grad = call(
        merge_body,
        [sds((model, units), BF16), sds((model, units), BF16), sds((units, model), BF16)],
        [kept, got],
        0,
        me,
    )
    layer_out, grad_tokens = call(
        combine_body,
        [sds((rows, width), BF16), sds((rows, width), BF16)],
        [pos, gate_probs, returned.reshape(copies * n, 2 * width)],
        8 * copies * n * rows * width,
    )
    return layer_out, grad_tokens, gate_grad[None], up_grad[None], down_grad[None]


def solution(mesh):
    experts = mesh.shape["expert"]
    fine = Mesh(mesh.devices.reshape(2, 2, 2, experts), (*DP, "expert"))
    return jax.shard_map(
        per_device,
        mesh=fine,
        in_specs=(
            P("expert", DP),
            P("expert", DP),
            P("expert", None),
            P("expert", None),
            P("expert", None, DP),
            P("expert", None, DP),
            P("expert", DP, None),
        ),
        out_specs=(
            P("expert", DP),
            P("expert", DP),
            P("expert", None, DP),
            P("expert", None, DP),
            P("expert", DP, None),
        ),
        check_vma=False,
    )
```
